32 devices in a mesh: orient: 16 (over z, y, core), frame: 2 (over x).
Axes of the slice: x: 2, y: 2, z: 4, core: 2. Of those that a mesh axis runs over, the one named last changes fastest.
Arguments:
- log_tomograms: bfloat16 [2048, 4096], P('orient'), may hold values from -3 to 3
- frames: int32 [512, 4096], P('frame'), may hold values from 0 to 15, as said below
- tile_index: int32 [2, 32, 2048], P(None, 'frame', 'orient'), may hold values from 0 to 383
- tile_weight: float32 [2, 32, 2048], P(None, 'frame', 'orient'), may hold values from 0.1 to 1
- prior_volume: float32 [2, 384, 128], P('frame', 'orient'), may hold values from 0.5 to 2
Outputs:
- new_log_tomograms: bfloat16 [2048, 4096], P('orient', 'frame')
- volume: float32 [2, 384, 128], P('frame', 'orient')
- evidence: float32 [512], P('frame')
The draws below stay inside these ranges and needn't reach their ends.
Inputs may be any that keep to these rules, and one draw needn't show every extreme that they name: `frames`: each frame's counts lie below a level of that frame; the first frame has a pixel with 15 photons. `tile_index`: the tile of an entry counts within the shell group of its pixel block.
All inputs are finite; a program needn't handle non-finite values.
Results may differ from the reference program's by a relative error of at most 0.008.
Values may be sent and summed in bfloat16 or wider, within the bound.
A program may use at most 64 MiB of HBM per device.

```python
import math
import jax
import jax.numpy as jnp
from jax import lax

PIX = 4096
TILE = 128
ROT_DEV = 128
FR_DEV = 256
TILE_DEV = 24
ORIENTS = 2048
FRAMES = 512
BLOCKS = 32
GROUPS = 2
TILES_COL = 384
N_ORIENT = 16
N_FRAME = 2


def frame_counts(key):
    level_key, count_key = jax.random.split(jax.random.fold_in(key, 11))
    levels = jax.random.randint(level_key, (FRAMES, 1), 1, 17)
    first_frame = jnp.arange(FRAMES)[:, None] == 0
    levels = jnp.where(first_frame, 16, levels)
    raw_bits = jax.random.randint(count_key, (FRAMES, PIX), 0, 1 << 20)
    counts = raw_bits % levels
    corner = first_frame & (jnp.arange(PIX)[None, :] == 0)
    counts = jnp.where(corner, 15, counts)
    return counts.astype(jnp.int32)


def draw_frames(key, part):
    return frame_counts(key)


def draw_log_tomograms(key, part):
    base_field = 0.5 * jax.random.normal(jax.random.fold_in(key, 23), (ORIENTS, PIX), jnp.float32)
    base_field = jnp.clip(base_field, -3.0, 3.0)
    return base_field.astype(jnp.bfloat16)


def touch_ends(values, stream_key, smallest, largest):
    longest = values.shape.index(max(values.shape))
    spots = []
    for shift in (0, 1):
        where = [jax.random.randint(jax.random.fold_in(stream_key, axis), (), 0, length) for axis, length in enumerate(values.shape)]
        where[longest] = (where[longest] + shift) % values.shape[longest]
        spots.append(tuple(where))
    return values.at[spots[0]].set(smallest).at[spots[1]].set(largest)


def block_scale(rng, dims, cuts, low, top_value):
    factor_of, own = 1.0, jax.random.fold_in(rng, 6)
    for dim, parts in cuts:
        steps = jnp.exp(jax.random.uniform(jax.random.fold_in(own, dim), (parts,), jnp.float32, low / len(cuts), top_value / len(cuts)))
        factor_of = factor_of * jnp.repeat(steps, dims[dim] // parts).reshape([-1 if axis == dim else 1 for axis in range(len(dims))])
    return factor_of


def setup_inputs(seed: int = 0) -> dict:
    keys = jax.random.split(jax.random.key(seed), 6)
    log_tomograms = draw_log_tomograms(jax.random.fold_in(keys[5], 71), 0)
    frames = draw_frames(jax.random.fold_in(keys[5], 71), 0)
    tile_index = touch_ends(jax.random.randint(keys[2], (2, BLOCKS, ORIENTS), 0, TILES_COL), jax.random.fold_in(keys[2], 1), 0, TILES_COL - 1).astype(jnp.int32)
    tile_weight = jnp.clip(jnp.exp(math.log(1.0) - 2.3025851 * jax.random.uniform(keys[3], (2, BLOCKS, ORIENTS), jnp.float32) ** block_scale(keys[3], (2, BLOCKS, ORIENTS), ((1, 2), (2, 16)), -0.2, 0.2)), 0.1, 1.0)
    prior_volume = jnp.clip(jnp.exp(math.log(2.0) - 1.3862944 * jax.random.uniform(keys[4], (GROUPS, TILES_COL, TILE), jnp.float32) ** block_scale(keys[4], (GROUPS, TILES_COL, TILE), ((0, 2), (1, 16)), -0.2, 0.2)), 0.5, 2.0)
    return {"log_tomograms": log_tomograms, "frames": frames, "tile_index": tile_index, "tile_weight": tile_weight, "prior_volume": prior_volume}


def reference(log_tomograms, frames, tile_index, tile_weight, prior_volume):
    inverse_temp = 64.0 / PIX
    counts = frames.astype(jnp.bfloat16)
    intensity = jnp.exp(log_tomograms.astype(jnp.float32))
    tomo_mass = jnp.sum(intensity, axis=1)
    correlation = jnp.dot(log_tomograms, counts.T, preferred_element_type=jnp.float32)
    scores = inverse_temp * (correlation - tomo_mass[:, None])
    score_peak = jnp.max(scores, axis=0)
    shifted = jnp.exp(scores - score_peak[None, :])
    score_total = jnp.sum(shifted, axis=0)
    responsibility = shifted / score_total[None, :]
    evidence = score_peak + jnp.log(score_total)
    resp_low = responsibility.astype(jnp.bfloat16)
    prior_share = (FR_DEV * N_FRAME) / (ROT_DEV * N_ORIENT)
    group_blocks = PIX // TILE // N_FRAME
    block_count = PIX // TILE
    tiles_column = TILE_DEV * N_ORIENT
    prior_weight = ROT_DEV * group_blocks / (4.0 * TILE_DEV)
    segment_base = (jnp.arange(block_count, dtype=jnp.int32) // group_blocks) * tiles_column

    def shard_update(first_row):
        numerator = jnp.zeros((ROT_DEV, PIX), jnp.float32)
        denominator = jnp.zeros((ROT_DEV,), jnp.float32)
        for frame_group in range(N_FRAME):
            column_first = jnp.int32(frame_group * FR_DEV)
            resp_part = lax.dynamic_slice(resp_low, (first_row, column_first), (ROT_DEV, FR_DEV))
            exact_part = lax.dynamic_slice(responsibility, (first_row, column_first), (ROT_DEV, FR_DEV))
            group_counts = counts[frame_group * FR_DEV:(frame_group + 1) * FR_DEV]
            numer_term = jnp.dot(resp_part, group_counts, preferred_element_type=jnp.float32)
            numer_term = lax.optimization_barrier(numer_term.astype(jnp.bfloat16)).astype(jnp.float32)
            denom_term = lax.optimization_barrier(jnp.sum(exact_part, axis=1).astype(jnp.bfloat16)).astype(jnp.float32)
            numerator = numerator + numer_term
            denominator = denominator + denom_term
        own_intensity = lax.dynamic_slice_in_dim(intensity, first_row, ROT_DEV, 0)
        return (numerator + prior_share * own_intensity) / (denominator[:, None] + prior_share)

    def shard_entries(first_row):
        shard_ids = lax.dynamic_slice_in_dim(tile_index, first_row, ROT_DEV, 2)
        shard_weight = lax.dynamic_slice_in_dim(tile_weight, first_row, ROT_DEV, 2)
        segment_ids = shard_ids + segment_base[None, :, None]
        return segment_ids, shard_weight

    def accumulate(running, shard_index):
        first_row = (shard_index * ROT_DEV).astype(jnp.int32)
        updated = shard_update(first_row)
        block_values = updated.reshape(ROT_DEV, block_count, TILE).transpose(1, 0, 2)
        segment_ids, shard_weight = shard_entries(first_row)
        contrib = shard_weight[..., None] * block_values[None]
        flat_ids = segment_ids.reshape(-1)
        numer_tiles = running[0] + jax.ops.segment_sum(contrib.reshape(-1, TILE), flat_ids, num_segments=N_FRAME * tiles_column)
        weight_tiles = running[1] + jax.ops.segment_sum(shard_weight.reshape(-1), flat_ids, num_segments=N_FRAME * tiles_column)
        return (numer_tiles, weight_tiles), None

    start_state = (jnp.zeros((N_FRAME * tiles_column, TILE), jnp.float32), jnp.zeros((N_FRAME * tiles_column,), jnp.float32))
    (numer_tiles, weight_tiles), _ = lax.scan(accumulate, start_state, jnp.arange(N_ORIENT, dtype=jnp.int32))
    prior_flat = prior_volume.reshape(N_FRAME * tiles_column, TILE)
    volume_flat = (numer_tiles + prior_weight * prior_flat) / (weight_tiles[:, None] + prior_weight)
    volume = volume_flat.reshape(N_FRAME, tiles_column, TILE)

    def slice_shard(shard_index):
        first_row = (shard_index * ROT_DEV).astype(jnp.int32)
        segment_ids, shard_weight = shard_entries(first_row)
        picked = volume_flat[segment_ids]
        blended = jnp.sum(shard_weight[..., None] * picked, axis=0) / jnp.sum(shard_weight, axis=0)[..., None]
        return jnp.log(blended).transpose(1, 0, 2).reshape(ROT_DEV, PIX).astype(jnp.bfloat16)

    new_log = lax.map(slice_shard, jnp.arange(N_ORIENT, dtype=jnp.int32)).reshape(ORIENTS, PIX)
    return (new_log, volume, evidence)
```

```python
import functools

import jax
import jax.numpy as jnp
from jax import lax
from jax.experimental import pallas as pl
from jax.experimental.pallas import tpu as pltpu
from jax.sharding import PartitionSpec as P

MESH = pl.DeviceIdType.MESH
F32 = jnp.float32
BF16 = jnp.bfloat16
PARTS = 4


def remote(src, dst, send_sem, recv_sem, where):
    return pltpu.make_async_remote_copy(
        src_ref=src,
        dst_ref=dst,
        send_sem=send_sem,
        recv_sem=recv_sem,
        device_id=where,
        device_id_type=MESH,
    )


def kernel(
    n_orient,
    n_frame,
    logt_hbm,
    frames_hbm,
    index_ref,
    weight_ref,
    prior_ref,
    new_log_ref,
    volume_ref,
    evidence_ref,
    logt,
    frames,
    counts,
    other,
    intensity,
    scores,
    stat_mine,
    stat_in,
    resp_out,
    resp_in,
    den_out,
    den_in,
    numer,
    spread,
    update,
    tile_out,
    tile_in,
    tiles,
    tiles_t,
    in_sem,
    count_send,
    count_recv,
    relay_send,
    relay_recv,
    resp_send,
    resp_recv,
    den_send,
    den_recv,
    fan_send,
    fan_recv,
):
    me = lax.axis_index("orient")
    mine = lax.axis_index("frame")
    rot_rows, pixels = logt.shape
    frame_rows = frames.shape[0]
    group_blocks = index_ref.shape[1]
    tile_rows, width = prior_ref.shape[1:]
    columns = pixels // n_frame
    tile_count = tile_rows * n_orient
    chunk = (384 // tile_rows if n_orient % max(384 // tile_rows, 1) == 0 else 1) * tile_rows
    core = lax.rem(me, 2)
    partner = me + 1 - 2 * core
    half = frame_rows // 2
    part = half // PARTS

    logt_copy = pltpu.make_async_copy(logt_hbm, logt, in_sem.at[0])
    logt_copy.start()
    step = frame_rows // PARTS
    frame_copies = []
    for c in range(PARTS):
        rows = pl.ds(c * step, step)
        copy = pltpu.make_async_copy(frames_hbm.at[rows], frames.at[rows], in_sem.at[1 + c])
        copy.start()
        frame_copies.append(copy)

    barrier = pltpu.get_barrier_semaphore()

    def greet(d, carry):
        pl.semaphore_signal(
            barrier, inc=1, device_id={"orient": lax.rem(me + d, n_orient)}, device_id_type=MESH
        )
        return carry

    lax.fori_loop(1, n_orient, greet, 0)
    for d in range(1, n_frame):
        pl.semaphore_signal(
            barrier, inc=1, device_id={"frame": lax.rem(mine + d, n_frame)}, device_id_type=MESH
        )

    for c in range(PARTS):
        frame_copies[c].wait()
        counts[c * step : (c + 1) * step] = (
            frames[c * step : (c + 1) * step].astype(F32).astype(BF16)
        )
    pl.semaphore_wait(barrier, n_orient - 1 + n_frame - 1)

    count_copies = []
    for d in range(1, n_frame):
        to = lax.rem(mine + d, n_frame)
        for c in range(PARTS):
            rows = pl.ds(pl.multiple_of(core * half + c * part, 16), part)
            copy = remote(
                counts.at[rows, pl.ds(pl.multiple_of(to * columns, 128), columns)],
                other.at[d - 1, rows],
                count_send.at[d - 1, c],
                count_recv.at[d - 1, c],
                {"frame": to},
            )
            copy.start()
            count_copies.append((d, c, copy))

    logt_copy.wait()
    mass = jnp.zeros((rot_rows, 128), F32)
    for c in range(pixels // 512):
        value = jnp.exp(logt[:, c * 512 : (c + 1) * 512].astype(F32))
        intensity[:, c * 512 : (c + 1) * 512] = value
        for k in range(4):
            mass = mass + value[:, k * 128 : (k + 1) * 128]
    mass = jnp.sum(mass, axis=1, keepdims=True)
    correlation = lax.dot_general(
        logt[...], counts[...], (((1,), (1,)), ((), ())), preferred_element_type=F32
    )
    score = (64.0 / pixels) * (correlation - mass)
    scores[...] = score
    peak = jnp.max(score, axis=0, keepdims=True)
    stat_mine[0:1, :] = peak
    stat_mine[1:2, :] = jnp.sum(jnp.exp(score - peak), axis=0, keepdims=True)

    def send_stat(d, carry):
        remote(
            stat_mine,
            stat_in.at[d - 1],
            fan_send.at[0],
            fan_recv.at[0],
            {"orient": lax.rem(me + d, n_orient)},
        ).start()
        return carry

    lax.fori_loop(1, n_orient, send_stat, 0)

    weight_low = weight_ref[...].astype(BF16).astype(F32)
    index = index_ref[...]
    lane = lax.broadcasted_iota(jnp.int32, (8, 128), 1)
    strip = tile_rows

    def build(o, carry):
        first = o * strip
        row_id = lax.broadcasted_iota(jnp.int32, (strip, rot_rows), 0) + first
        total = jnp.zeros((strip, rot_rows), F32)
        for j in range(group_blocks):
            value = jnp.where(row_id == index[0, j][None, :], weight_low[0, j][None, :], 0.0)
            value = value + jnp.where(
                row_id == index[1, j][None, :], weight_low[1, j][None, :], 0.0
            )
            low = value.astype(BF16)
            total = total + low.astype(F32)
            spread[o, :, j * rot_rows : (j + 1) * rot_rows] = low
        weight_sum = jnp.sum(total, axis=1, keepdims=True)
        packed = jnp.zeros((8, 128), F32)
        for b in range(tile_rows // 8):
            packed = packed + jnp.where(lane == b, weight_sum[b * 8 : (b + 1) * 8], 0.0)
        tile_out[o, tile_rows : tile_rows + 8] = packed
        return carry

    lax.fori_loop(0, n_orient, build, 0)

    fan_wait_recv = pltpu.make_async_copy(stat_in, stat_in, fan_recv.at[0])
    fan_wait_send = pltpu.make_async_copy(stat_in, stat_in, fan_send.at[0])
    fan_wait_recv.wait()
    peaks = stat_in[:, 0, :]
    totals = stat_in[:, 1, :]
    peak_mine = stat_mine[0:1, :]
    peak = jnp.maximum(jnp.max(peaks, axis=0, keepdims=True), peak_mine)
    total = stat_mine[1:2, :] * jnp.exp(peak_mine - peak) + jnp.sum(
        totals * jnp.exp(peaks - peak), axis=0, keepdims=True
    )
    evidence_ref[...] = peak + jnp.log(total)
    resp = jnp.exp(scores[...] - peak) / total
    resp_out[...] = resp.astype(BF16)
    den = jnp.sum(resp, axis=1, keepdims=True).astype(BF16)
    den_out[...] = jnp.broadcast_to(den, (rot_rows, 128))

    resp_copies = []
    for d in range(1, n_frame):
        to = {"frame": lax.rem(mine + d, n_frame)}
        copy = remote(resp_out, resp_in.at[d - 1], resp_send.at[d - 1], resp_recv.at[d - 1], to)
        copy.start()
        den_copy = remote(den_out, den_in.at[d - 1], den_send.at[d - 1], den_recv.at[d - 1], to)
        den_copy.start()
        resp_copies.append((copy, den_copy))
    fan_wait_send.wait()

    span = min(columns, 512)
    first = pl.multiple_of(mine * columns, 128)
    for c in range(columns // span):
        mixed = jnp.dot(
            resp_out[...],
            counts[:, pl.ds(pl.multiple_of(first + c * span, 128), span)],
            preferred_element_type=F32,
        )
        numer[:, c * span : (c + 1) * span] = mixed.astype(BF16).astype(F32)

    relay_copies = []
    for d, c, copy in count_copies:
        copy.wait_recv()
        rows = pl.ds(pl.multiple_of(core * half + c * part, 16), part)
        relay = remote(
            other.at[d - 1, rows],
            other.at[d - 1, rows],
            relay_send.at[d - 1, c],
            relay_recv.at[d - 1, c],
            {"orient": partner},
        )
        relay.start()
        relay_copies.append(relay)
    for copy, den_copy in resp_copies:
        copy.wait_recv()
        den_copy.wait_recv()
    for relay in relay_copies:
        relay.wait_recv()

    share = frame_rows * n_frame / (rot_rows * n_orient)
    den_all = den_out[...].astype(F32)
    for d in range(1, n_frame):
        den_all = den_all + den_in[d - 1].astype(F32)
    inverse = 1.0 / (den_all + share)
    for c in range(columns // span):
        cols = slice(c * span, (c + 1) * span)
        value = numer[:, cols]
        for d in range(1, n_frame):
            mixed = jnp.dot(resp_in[d - 1], other[d - 1, :, cols], preferred_element_type=F32)
            value = value + mixed.astype(BF16).astype(F32)
        value = value + share * intensity[:, pl.ds(pl.multiple_of(first + c * span, 128), span)]
        for k in range(span // width):
            j = c * (span // width) + k
            new = value[:, k * width : (k + 1) * width] * inverse
            high = new.astype(BF16)
            update[j * rot_rows : (j + 1) * rot_rows, 0:width] = high
            update[j * rot_rows : (j + 1) * rot_rows, width : 2 * width] = (
                new - high.astype(F32)
            ).astype(BF16)

    owners = chunk // tile_rows

    def gather_in(c, carry):
        block = spread[pl.ds(c * owners, owners)].reshape(chunk, group_blocks * rot_rows)
        summed = jnp.dot(block, update[...], preferred_element_type=F32)
        summed = summed[:, 0:width] + summed[:, width : 2 * width]
        for i in range(owners):
            tile_out[c * owners + i, 0:tile_rows] = summed[i * tile_rows : (i + 1) * tile_rows]
        return carry

    lax.fori_loop(0, tile_count // chunk, gather_in, 0)

    def send_tiles(d, carry):
        to = lax.rem(me + d, n_orient)
        remote(
            tile_out.at[to], tile_in.at[d - 1], fan_send.at[1], fan_recv.at[1], {"orient": to}
        ).start()
        return carry

    lax.fori_loop(1, n_orient, send_tiles, 0)
    pltpu.make_async_copy(tile_in, tile_in, fan_recv.at[1]).wait()
    whole = lax.fori_loop(0, n_orient - 1, lambda d, so_far: so_far + tile_in[d], tile_out[me])
    prior_weight = rot_rows * group_blocks / (4.0 * tile_rows)
    base = pl.multiple_of(me * tile_rows, 8)
    for b in range(tile_rows // 8):
        weight = whole[tile_rows : tile_rows + 8, b : b + 1]
        rows = slice(b * 8, (b + 1) * 8)
        value = (whole[rows] + prior_weight * prior_ref[0, rows]) / (weight + prior_weight)
        volume_ref[0, rows] = value
        tiles[pl.ds(base + b * 8, 8)] = value

    def send_volume(d, carry):
        own = tiles.at[pl.ds(base, tile_rows)]
        remote(
            own, own, fan_send.at[2], fan_recv.at[2], {"orient": lax.rem(me + d, n_orient)}
        ).start()
        return carry

    lax.fori_loop(1, n_orient, send_volume, 0)
    for d, c, copy in count_copies:
        copy.wait_send()
    for relay in relay_copies:
        relay.wait_send()
    for copy, den_copy in resp_copies:
        copy.wait_send()
        den_copy.wait_send()
    pltpu.make_async_copy(tile_in, tile_in, fan_send.at[1]).wait()
    incoming = tiles.at[pl.ds(0, tile_count - tile_rows)]
    pltpu.make_async_copy(incoming, incoming, fan_recv.at[2]).wait()

    def turn(c, carry):
        at = pl.multiple_of(c * 128, 128)
        value = tiles[pl.ds(at, 128)].T
        high = value.astype(BF16)
        tiles_t[0:width, pl.ds(at, 128)] = high
        tiles_t[width : 2 * width, pl.ds(at, 128)] = (value - high.astype(F32)).astype(BF16)
        return carry

    lax.fori_loop(0, tile_count // 128, turn, 0)
    both = weight_low[0] + weight_low[1]
    both = jnp.where(index[0] == index[1], both.astype(BF16).astype(F32), both)
    scale = 1.0 / both
    pair = 2 if group_blocks % 2 == 0 else 1
    for c in range(group_blocks // pair):
        cols = slice(c * pair * rot_rows, (c + 1) * pair * rot_rows)
        block = spread[:, :, cols].reshape(tile_count, pair * rot_rows)
        blended = jnp.dot(tiles_t[...], block, preferred_element_type=F32)
        blended = blended[0:width] + blended[width : 2 * width]
        for k in range(pair):
            j = c * pair + k
            value = jnp.log(blended[:, k * rot_rows : (k + 1) * rot_rows] * scale[j][None, :])
            new_log_ref[:, j * width : (j + 1) * width] = value.T.astype(BF16)
    pltpu.make_async_copy(incoming, incoming, fan_send.at[2]).wait()


def on_device(log_tomograms, frames, tile_index, tile_weight, prior_volume):
    n_orient = lax.axis_size("orient")
    n_frame = lax.axis_size("frame")
    rot_rows, pixels = log_tomograms.shape
    frame_rows = frames.shape[0]
    group_blocks = tile_index.shape[1]
    tile_rows, width = prior_volume.shape[1:]
    columns = pixels // n_frame
    tile_count = tile_rows * n_orient
    others = max(n_frame - 1, 1)
    dma = pltpu.SemaphoreType.DMA
    vmem = pl.BlockSpec(memory_space=pltpu.VMEM)
    anywhere = pl.BlockSpec(memory_space=pl.ANY)
    new_log, volume, evidence = pl.pallas_call(
        functools.partial(kernel, n_orient, n_frame),
        out_shape=(
            jax.ShapeDtypeStruct((rot_rows, columns), BF16),
            jax.ShapeDtypeStruct((1, tile_rows, width), F32),
            jax.ShapeDtypeStruct((1, frame_rows), F32),
        ),
        in_specs=[anywhere, anywhere, vmem, vmem, vmem],
        out_specs=(vmem, vmem, vmem),
        scratch_shapes=[
            pltpu.VMEM((rot_rows, pixels), BF16),
            pltpu.VMEM((frame_rows, pixels), jnp.int32),
            pltpu.VMEM((frame_rows, pixels), BF16),
            pltpu.VMEM((others, frame_rows, columns), BF16),
            pltpu.VMEM((rot_rows, pixels), F32),
            pltpu.VMEM((rot_rows, frame_rows), F32),
            pltpu.VMEM((2, frame_rows), F32),
            pltpu.VMEM((n_orient - 1, 2, frame_rows), F32),
            pltpu.VMEM((rot_rows, frame_rows), BF16),
            pltpu.VMEM((others, rot_rows, frame_rows), BF16),
            pltpu.VMEM((rot_rows, 128), BF16),
            pltpu.VMEM((others, rot_rows, 128), BF16),
            pltpu.VMEM((rot_rows, columns), F32),
            pltpu.VMEM((n_orient, tile_rows, group_blocks * rot_rows), BF16),
            pltpu.VMEM((group_blocks * rot_rows, 2 * width), BF16),
            pltpu.VMEM((n_orient, tile_rows + 8, width), F32),
            pltpu.VMEM((n_orient - 1, tile_rows + 8, width), F32),
            pltpu.VMEM((tile_count, width), F32),
            pltpu.VMEM((2 * width, tile_count), BF16),
            dma((1 + PARTS,)),
            dma((others, PARTS)),
            dma((others, PARTS)),
            dma((others, PARTS)),
            dma((others, PARTS)),
            dma((others,)),
            dma((others,)),
            dma((others,)),
            dma((others,)),
            dma((3,)),
            dma((3,)),
        ],
        compiler_params=pltpu.CompilerParams(
            collective_id=0, has_side_effects=True, vmem_limit_bytes=60 * 1024 * 1024
        ),
    )(log_tomograms, frames, tile_index, tile_weight, prior_volume)
    return (new_log, volume, evidence.reshape(frame_rows))


def solution(mesh):
    placed = (
        P("orient", None),
        P("frame", None),
        P(None, "frame", "orient"),
        P(None, "frame", "orient"),
        P("frame", "orient", None),
    )
    return jax.shard_map(
        on_device,
        mesh=mesh,
        in_specs=placed,
        out_specs=(P("orient", "frame"), P("frame", "orient", None), P("frame")),
        check_vma=False,
    )
```

```python
import functools

import jax
import jax.numpy as jnp
from jax import lax
from jax.experimental import pallas as pl
from jax.experimental.pallas import tpu as pltpu
from jax.sharding import PartitionSpec as P

MESH = pl.DeviceIdType.MESH
F32 = jnp.float32
BF16 = jnp.bfloat16
PARTS = 4


def remote(src, dst, send_sem, recv_sem, where):
    return pltpu.make_async_remote_copy(
        src_ref=src,
        dst_ref=dst,
        send_sem=send_sem,
        recv_sem=recv_sem,
        device_id=where,
        device_id_type=MESH,
    )


def kernel(
    n_orient,
    n_frame,
    logt_hbm,
    frames_hbm,
    index_hbm,
    weight_hbm,
    prior_hbm,
    new_log_ref,
    volume_ref,
    evidence_ref,
    logt,
    frames,
    index_ref,
    weight_ref,
    prior_ref,
    counts,
    other,
    intensity,
    scores,
    stat_mine,
    stat_in,
    resp_out,
    resp_in,
    den_out,
    den_in,
    numer,
    spread,
    update,
    tile_out,
    tile_in,
    tiles,
    tiles_t,
    in_sem,
    count_send,
    count_recv,
    relay_send,
    relay_recv,
    resp_send,
    resp_recv,
    den_send,
    den_recv,
    fan_send,
    fan_recv,
):
    me = lax.axis_index("orient")
    mine = lax.axis_index("frame")
    rot_rows, pixels = logt.shape
    frame_rows = frames.shape[0]
    group_blocks = index_ref.shape[1]
    tile_rows, width = prior_ref.shape[1:]
    columns = pixels // n_frame
    tile_count = tile_rows * n_orient
    chunk = (384 // tile_rows if n_orient % max(384 // tile_rows, 1) == 0 else 1) * tile_rows
    partner = me + 1 - 2 * lax.rem(me, 2)
    across = me + 2 - 4 * lax.rem(me // 2, 2)
    fourth = frame_rows // 4
    part = fourth // PARTS

    logt_copy = pltpu.make_async_copy(logt_hbm, logt, in_sem.at[0])
    logt_copy.start()
    step = frame_rows // PARTS
    frame_copies = []
    for c in range(PARTS):
        rows = pl.ds(c * step, step)
        copy = pltpu.make_async_copy(frames_hbm.at[rows], frames.at[rows], in_sem.at[1 + c])
        copy.start()
        frame_copies.append(copy)

    small_copies = []
    for i, (source, target) in enumerate(
        ((index_hbm, index_ref), (weight_hbm, weight_ref), (prior_hbm, prior_ref))
    ):
        copy = pltpu.make_async_copy(source, target, in_sem.at[1 + PARTS + i])
        copy.start()
        small_copies.append(copy)

    barrier = pltpu.get_barrier_semaphore()

    def greet(d, carry):
        pl.semaphore_signal(
            barrier, inc=1, device_id={"orient": lax.rem(me + d, n_orient)}, device_id_type=MESH
        )
        return carry

    lax.fori_loop(1, n_orient, greet, 0)
    for d in range(1, n_frame):
        pl.semaphore_signal(
            barrier, inc=1, device_id={"frame": lax.rem(mine + d, n_frame)}, device_id_type=MESH
        )

    for c in range(PARTS):
        frame_copies[c].wait()
        counts[c * step : (c + 1) * step] = (
            frames[c * step : (c + 1) * step].astype(F32).astype(BF16)
        )
    logt_copy.wait()
    mass = jnp.zeros((rot_rows, 128), F32)
    for c in range(pixels // 512):
        value = jnp.exp(logt[:, c * 512 : (c + 1) * 512].astype(F32))
        intensity[:, c * 512 : (c + 1) * 512] = value
        for k in range(4):
            mass = mass + value[:, k * 128 : (k + 1) * 128]
    mass = jnp.sum(mass, axis=1, keepdims=True)
    correlation = lax.dot_general(
        logt[...], counts[...], (((1,), (1,)), ((), ())), preferred_element_type=F32
    )
    score = (64.0 / pixels) * (correlation - mass)
    scores[...] = score
    peak = jnp.max(score, axis=0, keepdims=True)
    stat_mine[0:1, :] = peak
    stat_mine[1:2, :] = jnp.sum(jnp.exp(score - peak), axis=0, keepdims=True)

    pl.semaphore_wait(barrier, n_orient - 1 + n_frame - 1)

    def quarter(owner, c):
        return pl.ds(pl.multiple_of(lax.rem(owner, 4) * fourth + c * part, 16), part)

    count_copies = []
    for c in range(PARTS):
        for d in range(1, n_frame):
            to = lax.rem(mine + d, n_frame)
            copy = remote(
                counts.at[quarter(me, c), pl.ds(pl.multiple_of(to * columns, 128), columns)],
                other.at[d - 1, quarter(me, c)],
                count_send.at[d - 1, c],
                count_recv.at[d - 1, c],
                {"frame": to},
            )
            copy.start()
            count_copies.append((d, c, copy))

    def send_stat(d, carry):
        remote(
            stat_mine,
            stat_in.at[d - 1],
            fan_send.at[0],
            fan_recv.at[0],
            {"orient": lax.rem(me + d, n_orient)},
        ).start()
        return carry

    lax.fori_loop(1, n_orient, send_stat, 0)

    for copy in small_copies:
        copy.wait()

    weight_low = weight_ref[...].astype(BF16).astype(F32)
    index = index_ref[...]
    lane = lax.broadcasted_iota(jnp.int32, (8, 128), 1)
    joint = spread.shape[1] // tile_rows
    strip = joint * tile_rows

    def build(o, carry):
        first = o * strip
        row_id = lax.broadcasted_iota(jnp.int32, (strip, rot_rows), 0) + first
        total = jnp.zeros((strip, rot_rows), F32)
        for j in range(group_blocks):
            value = jnp.where(row_id == index[0, j][None, :], weight_low[0, j][None, :], 0.0)
            value = value + jnp.where(
                row_id == index[1, j][None, :], weight_low[1, j][None, :], 0.0
            )
            low = value.astype(BF16)
            total = total + low.astype(F32)
            spread[o, :, j * rot_rows : (j + 1) * rot_rows] = low
        weight_sum = jnp.sum(total, axis=1, keepdims=True)
        for i in range(joint):
            packed = jnp.zeros((8, 128), F32)
            for b in range(tile_rows // 8):
                at = i * tile_rows + b * 8
                packed = packed + jnp.where(lane == b, weight_sum[at : at + 8], 0.0)
            tile_out[o * joint + i, tile_rows : tile_rows + 8] = packed
        return carry

    lax.fori_loop(0, n_orient // joint, build, 0)

    relay_copies = []

    def relay(owner, d, c, kind, to):
        where = other.at[d - 1, quarter(owner, c)]
        copy = remote(
            where,
            where,
            relay_send.at[kind, d - 1, c],
            relay_recv.at[kind, d - 1, c],
            {"orient": to},
        )
        copy.start()
        relay_copies.append((kind, d, c, copy))

    def relay_first(start, stop):
        for d, c, copy in count_copies:
            if start <= c < stop:
                copy.wait_recv()
                relay(me, d, c, 0, across)
                relay(me, d, c, 1, partner)

    def relay_second(start, stop):
        for kind, d, c, copy in list(relay_copies):
            if kind == 0 and start <= c < stop:
                copy.wait_recv()
                relay(across, d, c, 2, partner)

    relay_first(0, 2)

    fan_wait_recv = pltpu.make_async_copy(stat_in, stat_in, fan_recv.at[0])
    fan_wait_send = pltpu.make_async_copy(stat_in, stat_in, fan_send.at[0])
    fan_wait_recv.wait()
    peaks = stat_in[:, 0, :]
    totals = stat_in[:, 1, :]
    peak_mine = stat_mine[0:1, :]
    peak = jnp.maximum(jnp.max(peaks, axis=0, keepdims=True), peak_mine)
    total = stat_mine[1:2, :] * jnp.exp(peak_mine - peak) + jnp.sum(
        totals * jnp.exp(peaks - peak), axis=0, keepdims=True
    )
    evidence_ref[...] = peak + jnp.log(total)
    resp = jnp.exp(scores[...] - peak) / total
    resp_out[...] = resp.astype(BF16)
    den = jnp.sum(resp, axis=1, keepdims=True).astype(BF16)
    den_out[...] = jnp.broadcast_to(den, (rot_rows, 128))

    resp_copies = []
    for d in range(1, n_frame):
        to = {"frame": lax.rem(mine + d, n_frame)}
        copy = remote(resp_out, resp_in.at[d - 1], resp_send.at[d - 1], resp_recv.at[d - 1], to)
        copy.start()
        den_copy = remote(den_out, den_in.at[d - 1], den_send.at[d - 1], den_recv.at[d - 1], to)
        den_copy.start()
        resp_copies.append((copy, den_copy))
    fan_wait_send.wait()

    span = min(columns, 512)
    first = pl.multiple_of(mine * columns, 128)
    for c in range(columns // span):
        mixed = jnp.dot(
            resp_out[...],
            counts[:, pl.ds(pl.multiple_of(first + c * span, 128), span)],
            preferred_element_type=F32,
        )
        numer[:, c * span : (c + 1) * span] = mixed.astype(BF16).astype(F32)

    relay_first(2, PARTS)
    relay_second(0, PARTS)
    for copy, den_copy in resp_copies:
        copy.wait_recv()
        den_copy.wait_recv()
    for kind, d, c, copy in relay_copies:
        if kind > 0:
            copy.wait_recv()

    share = frame_rows * n_frame / (rot_rows * n_orient)
    den_all = den_out[...].astype(F32)
    for d in range(1, n_frame):
        den_all = den_all + den_in[d - 1].astype(F32)
    inverse = 1.0 / (den_all + share)
    for c in range(columns // span):
        cols = slice(c * span, (c + 1) * span)
        value = numer[:, cols]
        for d in range(1, n_frame):
            mixed = jnp.dot(resp_in[d - 1], other[d - 1, :, cols], preferred_element_type=F32)
            value = value + mixed.astype(BF16).astype(F32)
        value = value + share * intensity[:, pl.ds(pl.multiple_of(first + c * span, 128), span)]
        for k in range(span // width):
            j = c * (span // width) + k
            new = value[:, k * width : (k + 1) * width] * inverse
            high = new.astype(BF16)
            update[j * rot_rows : (j + 1) * rot_rows, 0:width] = high
            update[j * rot_rows : (j + 1) * rot_rows, width : 2 * width] = (
                new - high.astype(F32)
            ).astype(BF16)

    owners = chunk // tile_rows

    def gather_in(c, carry):
        block = spread[pl.ds(c * (chunk // strip), chunk // strip)].reshape(chunk, group_blocks * rot_rows)
        summed = jnp.dot(block, update[...], preferred_element_type=F32)
        summed = summed[:, 0:width] + summed[:, width : 2 * width]
        for i in range(owners):
            tile_out[c * owners + i, 0:tile_rows] = summed[i * tile_rows : (i + 1) * tile_rows]
        return carry

    lax.fori_loop(0, tile_count // chunk, gather_in, 0)

    def send_tiles(d, carry):
        to = lax.rem(me + d, n_orient)
        remote(
            tile_out.at[to], tile_in.at[d - 1], fan_send.at[1], fan_recv.at[1], {"orient": to}
        ).start()
        return carry

    lax.fori_loop(1, n_orient, send_tiles, 0)
    pltpu.make_async_copy(tile_in, tile_in, fan_recv.at[1]).wait()
    whole = lax.fori_loop(0, n_orient - 1, lambda d, so_far: so_far + tile_in[d], tile_out[me])
    prior_weight = rot_rows * group_blocks / (4.0 * tile_rows)
    base = pl.multiple_of(me * tile_rows, 8)
    for b in range(tile_rows // 8):
        weight = whole[tile_rows : tile_rows + 8, b : b + 1]
        rows = slice(b * 8, (b + 1) * 8)
        value = (whole[rows] + prior_weight * prior_ref[0, rows]) / (weight + prior_weight)
        volume_ref[0, rows] = value
        tiles[pl.ds(base + b * 8, 8)] = value

    def send_volume(d, carry):
        own = tiles.at[pl.ds(base, tile_rows)]
        remote(
            own, own, fan_send.at[2], fan_recv.at[2], {"orient": lax.rem(me + d, n_orient)}
        ).start()
        return carry

    lax.fori_loop(1, n_orient, send_volume, 0)
    for d, c, copy in count_copies:
        copy.wait_send()
    for kind, d, c, copy in relay_copies:
        copy.wait_send()
    for copy, den_copy in resp_copies:
        copy.wait_send()
        den_copy.wait_send()
    pltpu.make_async_copy(tile_in, tile_in, fan_send.at[1]).wait()
    incoming = tiles.at[pl.ds(0, tile_count - tile_rows)]
    pltpu.make_async_copy(incoming, incoming, fan_recv.at[2]).wait()

    def turn(c, carry):
        at = pl.multiple_of(c * 128, 128)
        value = tiles[pl.ds(at, 128)].T
        high = value.astype(BF16)
        tiles_t[0:width, pl.ds(at, 128)] = high
        tiles_t[width : 2 * width, pl.ds(at, 128)] = (value - high.astype(F32)).astype(BF16)
        return carry

    lax.fori_loop(0, tile_count // 128, turn, 0)
    both = weight_low[0] + weight_low[1]
    both = jnp.where(index[0] == index[1], both.astype(BF16).astype(F32), both)
    scale = 1.0 / both
    pair = 2 if group_blocks % 2 == 0 else 1
    for c in range(group_blocks // pair):
        cols = slice(c * pair * rot_rows, (c + 1) * pair * rot_rows)
        block = spread[:, :, cols].reshape(tile_count, pair * rot_rows)
        blended = jnp.dot(tiles_t[...], block, preferred_element_type=F32)
        blended = blended[0:width] + blended[width : 2 * width]
        for k in range(pair):
            j = c * pair + k
            value = jnp.log(blended[:, k * rot_rows : (k + 1) * rot_rows] * scale[j][None, :])
            new_log_ref[:, j * width : (j + 1) * width] = value.T.astype(BF16)
    pltpu.make_async_copy(incoming, incoming, fan_send.at[2]).wait()


def place(a_in, b_in, c_in, a_out, b_out, c_out, sem):
    copies = [
        pltpu.make_async_copy(source, target, sem.at[i])
        for i, (source, target) in enumerate(((a_in, a_out), (b_in, b_out), (c_in, c_out)))
    ]
    for copy in copies:
        copy.start()
    for copy in copies:
        copy.wait()


def on_device(log_tomograms, frames, tile_index, tile_weight, prior_volume):
    n_orient = lax.axis_size("orient")
    n_frame = lax.axis_size("frame")
    rot_rows, pixels = log_tomograms.shape
    frame_rows = frames.shape[0]
    group_blocks = tile_index.shape[1]
    tile_rows, width = prior_volume.shape[1:]
    columns = pixels // n_frame
    tile_count = tile_rows * n_orient
    others = max(n_frame - 1, 1)
    dma = pltpu.SemaphoreType.DMA
    vmem = pl.BlockSpec(memory_space=pltpu.VMEM)
    hbm = pl.BlockSpec(memory_space=pltpu.HBM)
    new_log, volume, evidence = pl.pallas_call(
        functools.partial(kernel, n_orient, n_frame),
        out_shape=(
            pltpu.VMEM((rot_rows, columns), BF16),
            pltpu.VMEM((1, tile_rows, width), F32),
            pltpu.VMEM((1, frame_rows), F32),
        ),
        in_specs=[hbm] * 5,
        out_specs=(vmem, vmem, vmem),
        scratch_shapes=[
            pltpu.VMEM((rot_rows, pixels), BF16),
            pltpu.VMEM((frame_rows, pixels), jnp.int32),
            pltpu.VMEM(tile_index.shape, jnp.int32),
            pltpu.VMEM(tile_weight.shape, F32),
            pltpu.VMEM(prior_volume.shape, F32),
            pltpu.VMEM((frame_rows, pixels), BF16),
            pltpu.VMEM((others, frame_rows, columns), BF16),
            pltpu.VMEM((rot_rows, pixels), F32),
            pltpu.VMEM((rot_rows, frame_rows), F32),
            pltpu.VMEM((2, frame_rows), F32),
            pltpu.VMEM((n_orient - 1, 2, frame_rows), F32),
            pltpu.VMEM((rot_rows, frame_rows), BF16),
            pltpu.VMEM((others, rot_rows, frame_rows), BF16),
            pltpu.VMEM((rot_rows, 128), BF16),
            pltpu.VMEM((others, rot_rows, 128), BF16),
            pltpu.VMEM((rot_rows, columns), F32),
            pltpu.VMEM((n_orient // 2, 2 * tile_rows, group_blocks * rot_rows), BF16),
            pltpu.VMEM((group_blocks * rot_rows, 2 * width), BF16),
            pltpu.VMEM((n_orient, tile_rows + 8, width), F32),
            pltpu.VMEM((n_orient - 1, tile_rows + 8, width), F32),
            pltpu.VMEM((tile_count, width), F32),
            pltpu.VMEM((2 * width, tile_count), BF16),
            dma((4 + PARTS,)),
            dma((others, PARTS)),
            dma((others, PARTS)),
            dma((3, others, PARTS)),
            dma((3, others, PARTS)),
            dma((others,)),
            dma((others,)),
            dma((others,)),
            dma((others,)),
            dma((3,)),
            dma((3,)),
        ],
        compiler_params=pltpu.CompilerParams(
            collective_id=0, has_side_effects=True, vmem_limit_bytes=48 * 1024 * 1024
        ),
    )(*(
        pltpu.with_memory_space_constraint(value, pltpu.HBM)
        for value in (log_tomograms, frames, tile_index, tile_weight, prior_volume)
    ))
    made = (new_log, volume, evidence)
    new_log, volume, evidence = pl.pallas_call(
        place,
        out_shape=tuple(jax.ShapeDtypeStruct(value.shape, value.dtype) for value in made),
        in_specs=[vmem] * 3,
        out_specs=(hbm,) * 3,
        scratch_shapes=[dma((3,))],
        compiler_params=pltpu.CompilerParams(vmem_limit_bytes=4 * 1024 * 1024),
    )(*made)
    return (new_log, volume, evidence.reshape(frame_rows))


def solution(mesh):
    placed = (
        P("orient", None),
        P("frame", None),
        P(None, "frame", "orient"),
        P(None, "frame", "orient"),
        P("frame", "orient", None),
    )
    return jax.shard_map(
        on_device,
        mesh=mesh,
        in_specs=placed,
        out_specs=(P("orient", "frame"), P("frame", "orient", None), P("frame")),
        check_vma=False,
    )
```

```python
import functools

import jax
import jax.numpy as jnp
from jax import lax
from jax.experimental import pallas as pl
from jax.experimental.pallas import tpu as pltpu
from jax.sharding import PartitionSpec as P

MESH = pl.DeviceIdType.MESH
F32 = jnp.float32
BF16 = jnp.bfloat16
PARTS = 4


def remote(src, dst, send_sem, recv_sem, where):
    return pltpu.make_async_remote_copy(
        src_ref=src,
        dst_ref=dst,
        send_sem=send_sem,
        recv_sem=recv_sem,
        device_id=where,
        device_id_type=MESH,
    )


def kernel(
    n_orient,
    n_frame,
    logt_hbm,
    frames_hbm,
    index_hbm,
    weight_hbm,
    prior_hbm,
    new_log_ref,
    volume_ref,
    evidence_ref,
    logt,
    frames,
    index_ref,
    weight_ref,
    prior_ref,
    counts,
    other,
    intensity,
    scores,
    stat_mine,
    stat_in,
    resp_out,
    resp_in,
    den_out,
    den_in,
    numer,
    spread,
    update,
    sums,
    tile_out,
    tile_in,
    tiles,
    tiles_t,
    in_sem,
    count_send,
    count_recv,
    relay_send,
    relay_recv,
    resp_send,
    resp_recv,
    den_send,
    den_recv,
    fan_send,
    fan_recv,
):
    me = lax.axis_index("orient")
    mine = lax.axis_index("frame")
    rot_rows, pixels = logt.shape
    frame_rows = frames.shape[0]
    group_blocks = index_ref.shape[1]
    tile_rows, width = prior_ref.shape[1:]
    columns = pixels // n_frame
    tile_count = tile_rows * n_orient
    chunk = (384 // tile_rows if n_orient % max(384 // tile_rows, 1) == 0 else 1) * tile_rows
    partner = me + 1 - 2 * lax.rem(me, 2)
    across = me + 2 - 4 * lax.rem(me // 2, 2)
    fourth = frame_rows // 4
    part = fourth // PARTS

    logt_copy = pltpu.make_async_copy(logt_hbm, logt, in_sem.at[0])
    logt_copy.start()
    step = frame_rows // PARTS
    frame_copies = []
    for c in range(PARTS):
        rows = pl.ds(c * step, step)
        copy = pltpu.make_async_copy(frames_hbm.at[rows], frames.at[rows], in_sem.at[1 + c])
        copy.start()
        frame_copies.append(copy)

    small_copies = []
    for i, (source, target) in enumerate(
        ((index_hbm, index_ref), (weight_hbm, weight_ref), (prior_hbm, prior_ref))
    ):
        copy = pltpu.make_async_copy(source, target, in_sem.at[1 + PARTS + i])
        copy.start()
        small_copies.append(copy)

    barrier = pltpu.get_barrier_semaphore()

    def greet(d, carry):
        pl.semaphore_signal(
            barrier, inc=1, device_id={"orient": lax.rem(me + d, n_orient)}, device_id_type=MESH
        )
        return carry

    lax.fori_loop(1, n_orient, greet, 0)
    for d in range(1, n_frame):
        pl.semaphore_signal(
            barrier, inc=1, device_id={"frame": lax.rem(mine + d, n_frame)}, device_id_type=MESH
        )

    for c in range(PARTS):
        frame_copies[c].wait()
        counts[c * step : (c + 1) * step] = (
            frames[c * step : (c + 1) * step].astype(F32).astype(BF16)
        )
    logt_copy.wait()
    mass = jnp.zeros((rot_rows, 128), F32)
    for c in range(pixels // 512):
        value = jnp.exp(logt[:, c * 512 : (c + 1) * 512].astype(F32))
        intensity[:, c * 512 : (c + 1) * 512] = value
        for k in range(4):
            mass = mass + value[:, k * 128 : (k + 1) * 128]
    mass = jnp.sum(mass, axis=1, keepdims=True)
    correlation = lax.dot_general(
        logt[...], counts[...], (((1,), (1,)), ((), ())), preferred_element_type=F32
    )
    score = (64.0 / pixels) * (correlation - mass)
    scores[...] = score
    peak = jnp.max(score, axis=0, keepdims=True)
    stat_mine[0:1, :] = peak
    stat_mine[1:2, :] = jnp.sum(jnp.exp(score - peak), axis=0, keepdims=True)

    pl.semaphore_wait(barrier, n_orient - 1 + n_frame - 1)

    def quarter(owner, c):
        return pl.ds(pl.multiple_of(lax.rem(owner, 4) * fourth + c * part, 16), part)

    count_copies = []
    for c in range(PARTS):
        for d in range(1, n_frame):
            to = lax.rem(mine + d, n_frame)
            copy = remote(
                counts.at[quarter(me, c), pl.ds(pl.multiple_of(to * columns, 128), columns)],
                other.at[d - 1, quarter(me, c)],
                count_send.at[d - 1, c],
                count_recv.at[d - 1, c],
                {"frame": to},
            )
            copy.start()
            count_copies.append((d, c, copy))

    def send_stat(d, carry):
        remote(
            stat_mine,
            stat_in.at[d - 1],
            fan_send.at[0],
            fan_recv.at[0],
            {"orient": lax.rem(me + d, n_orient)},
        ).start()
        return carry

    lax.fori_loop(1, n_orient, send_stat, 0)

    for copy in small_copies:
        copy.wait()

    weight_low = weight_ref[...].astype(BF16).astype(F32)
    index = index_ref[...]
    lane = lax.broadcasted_iota(jnp.int32, (8, 128), 1)
    joint = spread.shape[1] // tile_rows
    strip = joint * tile_rows

    def build(o, carry):
        first = o * strip
        row_id = lax.broadcasted_iota(jnp.int32, (strip, rot_rows), 0) + first
        total = jnp.zeros((strip, rot_rows), F32)
        for j in range(group_blocks):
            value = jnp.where(row_id == index[0, j][None, :], weight_low[0, j][None, :], 0.0)
            value = value + jnp.where(
                row_id == index[1, j][None, :], weight_low[1, j][None, :], 0.0
            )
            low = value.astype(BF16)
            total = total + low.astype(F32)
            spread[o, :, j * rot_rows : (j + 1) * rot_rows] = low
        weight_sum = jnp.sum(total, axis=1, keepdims=True)
        for i in range(joint):
            packed = jnp.zeros((8, 128), F32)
            for b in range(tile_rows // 8):
                at = i * tile_rows + b * 8
                exact = weight_sum[at : at + 8]
                high = exact.astype(BF16).astype(F32)
                packed = packed + jnp.where(lane == b, high, 0.0)
                packed = packed + jnp.where(lane == 64 + b, exact - high, 0.0)
            sums[o * joint + i] = packed
        return carry

    lax.fori_loop(0, n_orient // joint, build, 0)

    relay_copies = []

    def relay(owner, d, c, kind, to):
        where = other.at[d - 1, quarter(owner, c)]
        copy = remote(
            where,
            where,
            relay_send.at[kind, d - 1, c],
            relay_recv.at[kind, d - 1, c],
            {"orient": to},
        )
        copy.start()
        relay_copies.append((kind, d, c, copy))

    def relay_first(start, stop):
        for d, c, copy in count_copies:
            if start <= c < stop:
                copy.wait_recv()
                relay(me, d, c, 0, across)
                relay(me, d, c, 1, partner)

    def relay_second(start, stop):
        for kind, d, c, copy in list(relay_copies):
            if kind == 0 and start <= c < stop:
                copy.wait_recv()
                relay(across, d, c, 2, partner)

    relay_first(0, 2)

    fan_wait_recv = pltpu.make_async_copy(stat_in, stat_in, fan_recv.at[0])
    fan_wait_send = pltpu.make_async_copy(stat_in, stat_in, fan_send.at[0])
    fan_wait_recv.wait()
    peaks = stat_in[:, 0, :]
    totals = stat_in[:, 1, :]
    peak_mine = stat_mine[0:1, :]
    peak = jnp.maximum(jnp.max(peaks, axis=0, keepdims=True), peak_mine)
    total = stat_mine[1:2, :] * jnp.exp(peak_mine - peak) + jnp.sum(
        totals * jnp.exp(peaks - peak), axis=0, keepdims=True
    )
    evidence_ref[...] = peak + jnp.log(total)
    resp = jnp.exp(scores[...] - peak) / total
    resp_out[...] = resp.astype(BF16)
    den = jnp.sum(resp, axis=1, keepdims=True).astype(BF16)
    den_out[...] = jnp.broadcast_to(den, (rot_rows, 128))

    resp_copies = []
    for d in range(1, n_frame):
        to = {"frame": lax.rem(mine + d, n_frame)}
        copy = remote(resp_out, resp_in.at[d - 1], resp_send.at[d - 1], resp_recv.at[d - 1], to)
        copy.start()
        den_copy = remote(den_out, den_in.at[d - 1], den_send.at[d - 1], den_recv.at[d - 1], to)
        den_copy.start()
        resp_copies.append((copy, den_copy))
    fan_wait_send.wait()

    span = min(columns, 512)
    first = pl.multiple_of(mine * columns, 128)
    for c in range(columns // span):
        mixed = jnp.dot(
            resp_out[...],
            counts[:, pl.ds(pl.multiple_of(first + c * span, 128), span)],
            preferred_element_type=F32,
        )
        numer[:, c * span : (c + 1) * span] = mixed.astype(BF16).astype(F32)

    relay_first(2, PARTS)
    relay_second(0, PARTS)
    for copy, den_copy in resp_copies:
        copy.wait_recv()
        den_copy.wait_recv()
    for kind, d, c, copy in relay_copies:
        if kind > 0:
            copy.wait_recv()

    share = frame_rows * n_frame / (rot_rows * n_orient)
    den_all = den_out[...].astype(F32)
    for d in range(1, n_frame):
        den_all = den_all + den_in[d - 1].astype(F32)
    inverse = 1.0 / (den_all + share)
    for c in range(columns // span):
        cols = slice(c * span, (c + 1) * span)
        value = numer[:, cols]
        for d in range(1, n_frame):
            mixed = jnp.dot(resp_in[d - 1], other[d - 1, :, cols], preferred_element_type=F32)
            value = value + mixed.astype(BF16).astype(F32)
        value = value + share * intensity[:, pl.ds(pl.multiple_of(first + c * span, 128), span)]
        for k in range(span // width):
            j = c * (span // width) + k
            new = value[:, k * width : (k + 1) * width] * inverse
            high = new.astype(BF16)
            update[j * rot_rows : (j + 1) * rot_rows, 0:width] = high
            update[j * rot_rows : (j + 1) * rot_rows, width : 2 * width] = (
                new - high.astype(F32)
            ).astype(BF16)

    owners = chunk // tile_rows

    def gather_in(c, carry):
        block = spread[pl.ds(c * (chunk // strip), chunk // strip)].reshape(chunk, group_blocks * rot_rows)
        summed = jnp.dot(block, update[...], preferred_element_type=F32)
        summed = summed[:, 0:width] + summed[:, width : 2 * width]
        for i in range(owners):
            own = summed[i * tile_rows : (i + 1) * tile_rows]
            message = jnp.concatenate([own, sums[c * owners + i]], axis=0)
            tile_out[c * owners + i] = message.astype(BF16)
        return carry

    lax.fori_loop(0, tile_count // chunk, gather_in, 0)

    def send_tiles(d, carry):
        to = lax.rem(me + d, n_orient)
        remote(
            tile_out.at[to], tile_in.at[d - 1], fan_send.at[1], fan_recv.at[1], {"orient": to}
        ).start()
        return carry

    lax.fori_loop(1, n_orient, send_tiles, 0)
    pltpu.make_async_copy(tile_in, tile_in, fan_recv.at[1]).wait()
    whole = lax.fori_loop(0, n_orient - 1, lambda d, so_far: so_far + tile_in[d].astype(F32), tile_out[me].astype(F32))
    prior_weight = rot_rows * group_blocks / (4.0 * tile_rows)
    weight = [
        whole[tile_rows:, b : b + 1] + whole[tile_rows:, 64 + b : 65 + b]
        for b in range(tile_rows // 8)
    ]
    weight = jnp.concatenate(weight, axis=0)
    value = whole[0:tile_rows] + prior_weight * prior_ref[0]
    value = value / (weight + prior_weight)
    volume_ref[0] = value
    tiles[me] = (value - 1.0).astype(BF16)

    def send_volume(d, carry):
        own = tiles.at[me]
        remote(
            own, own, fan_send.at[2], fan_recv.at[2], {"orient": lax.rem(me + d, n_orient)}
        ).start()
        return carry

    lax.fori_loop(1, n_orient, send_volume, 0)
    for d, c, copy in count_copies:
        copy.wait_send()
    for kind, d, c, copy in relay_copies:
        copy.wait_send()
    for copy, den_copy in resp_copies:
        copy.wait_send()
        den_copy.wait_send()
    pltpu.make_async_copy(tile_in, tile_in, fan_send.at[1]).wait()
    incoming = tiles.at[pl.ds(0, n_orient - 1)]
    pltpu.make_async_copy(incoming, incoming, fan_recv.at[2]).wait()

    def turn(c, carry):
        value = tiles[pl.ds(c * owners, owners)].astype(F32).reshape(chunk, width)
        tiles_t[:, pl.ds(pl.multiple_of(c * chunk, 128), chunk)] = value.T.astype(BF16)
        return carry

    lax.fori_loop(0, tile_count // chunk, turn, 0)
    both = weight_low[0] + weight_low[1]
    both = jnp.where(index[0] == index[1], both.astype(BF16).astype(F32), both)
    scale = 1.0 / both
    pair = 2 if group_blocks % 2 == 0 else 1
    for c in range(group_blocks // pair):
        cols = slice(c * pair * rot_rows, (c + 1) * pair * rot_rows)
        block = spread[:, :, cols].reshape(tile_count, pair * rot_rows)
        blended = jnp.dot(tiles_t[...], block, preferred_element_type=F32)
        for k in range(pair):
            j = c * pair + k
            value = blended[:, k * rot_rows : (k + 1) * rot_rows] * scale[j][None, :]
            value = jnp.log(1.0 + value)
            new_log_ref[:, j * width : (j + 1) * width] = value.T.astype(BF16)
    pltpu.make_async_copy(incoming, incoming, fan_send.at[2]).wait()


def place(a_in, b_in, c_in, a_out, b_out, c_out, sem):
    copies = [
        pltpu.make_async_copy(source, target, sem.at[i])
        for i, (source, target) in enumerate(((a_in, a_out), (b_in, b_out), (c_in, c_out)))
    ]
    for copy in copies:
        copy.start()
    for copy in copies:
        copy.wait()


def on_device(log_tomograms, frames, tile_index, tile_weight, prior_volume):
    n_orient = lax.axis_size("orient")
    n_frame = lax.axis_size("frame")
    rot_rows, pixels = log_tomograms.shape
    frame_rows = frames.shape[0]
    group_blocks = tile_index.shape[1]
    tile_rows, width = prior_volume.shape[1:]
    columns = pixels // n_frame
    tile_count = tile_rows * n_orient
    others = max(n_frame - 1, 1)
    dma = pltpu.SemaphoreType.DMA
    vmem = pl.BlockSpec(memory_space=pltpu.VMEM)
    hbm = pl.BlockSpec(memory_space=pltpu.HBM)
    new_log, volume, evidence = pl.pallas_call(
        functools.partial(kernel, n_orient, n_frame),
        out_shape=(
            pltpu.VMEM((rot_rows, columns), BF16),
            pltpu.VMEM((1, tile_rows, width), F32),
            pltpu.VMEM((1, frame_rows), F32),
        ),
        in_specs=[hbm] * 5,
        out_specs=(vmem, vmem, vmem),
        scratch_shapes=[
            pltpu.VMEM((rot_rows, pixels), BF16),
            pltpu.VMEM((frame_rows, pixels), jnp.int32),
            pltpu.VMEM(tile_index.shape, jnp.int32),
            pltpu.VMEM(tile_weight.shape, F32),
            pltpu.VMEM(prior_volume.shape, F32),
            pltpu.VMEM((frame_rows, pixels), BF16),
            pltpu.VMEM((others, frame_rows, columns), BF16),
            pltpu.VMEM((rot_rows, pixels), F32),
            pltpu.VMEM((rot_rows, frame_rows), F32),
            pltpu.VMEM((2, frame_rows), F32),
            pltpu.VMEM((n_orient - 1, 2, frame_rows), F32),
            pltpu.VMEM((rot_rows, frame_rows), BF16),
            pltpu.VMEM((others, rot_rows, frame_rows), BF16),
            pltpu.VMEM((rot_rows, 128), BF16),
            pltpu.VMEM((others, rot_rows, 128), BF16),
            pltpu.VMEM((rot_rows, columns), F32),
            pltpu.VMEM((n_orient // 2, 2 * tile_rows, group_blocks * rot_rows), BF16),
            pltpu.VMEM((group_blocks * rot_rows, 2 * width), BF16),
            pltpu.VMEM((n_orient, 8, width), F32),
            pltpu.VMEM((n_orient, tile_rows + 8, width), BF16),
            pltpu.VMEM((n_orient - 1, tile_rows + 8, width), BF16),
            pltpu.VMEM((n_orient, tile_rows, width), BF16),
            pltpu.VMEM((width, tile_count), BF16),
            dma((4 + PARTS,)),
            dma((others, PARTS)),
            dma((others, PARTS)),
            dma((3, others, PARTS)),
            dma((3, others, PARTS)),
            dma((others,)),
            dma((others,)),
            dma((others,)),
            dma((others,)),
            dma((3,)),
            dma((3,)),
        ],
        compiler_params=pltpu.CompilerParams(
            collective_id=0, has_side_effects=True, vmem_limit_bytes=48 * 1024 * 1024
        ),
    )(*(
        pltpu.with_memory_space_constraint(value, pltpu.HBM)
        for value in (log_tomograms, frames, tile_index, tile_weight, prior_volume)
    ))
    made = (new_log, volume, evidence)
    new_log, volume, evidence = pl.pallas_call(
        place,
        out_shape=tuple(jax.ShapeDtypeStruct(value.shape, value.dtype) for value in made),
        in_specs=[vmem] * 3,
        out_specs=(hbm,) * 3,
        scratch_shapes=[dma((3,))],
        compiler_params=pltpu.CompilerParams(vmem_limit_bytes=4 * 1024 * 1024),
    )(*made)
    return (new_log, volume, evidence.reshape(frame_rows))


def solution(mesh):
    placed = (
        P("orient", None),
        P("frame", None),
        P(None, "frame", "orient"),
        P(None, "frame", "orient"),
        P("frame", "orient", None),
    )
    return jax.shard_map(
        on_device,
        mesh=mesh,
        in_specs=placed,
        out_specs=(P("orient", "frame"), P("frame", "orient", None), P("frame")),
        check_vma=False,
    )
```

```python
import functools

import jax
import jax.numpy as jnp
from jax import lax
from jax.experimental import pallas as pl
from jax.experimental.pallas import tpu as pltpu
from jax.sharding import PartitionSpec as P

MESH = pl.DeviceIdType.MESH
F32 = jnp.float32
BF16 = jnp.bfloat16
PARTS = 4


def remote(src, dst, send_sem, recv_sem, where):
    return pltpu.make_async_remote_copy(
        src_ref=src,
        dst_ref=dst,
        send_sem=send_sem,
        recv_sem=recv_sem,
        device_id=where,
        device_id_type=MESH,
    )


def kernel(
    n_orient,
    n_frame,
    logt_hbm,
    frames_hbm,
    index_hbm,
    weight_hbm,
    prior_hbm,
    new_log_ref,
    volume_ref,
    evidence_ref,
    logt,
    frames,
    index_ref,
    weight_ref,
    prior_ref,
    counts,
    other,
    intensity,
    scores,
    stat_mine,
    stat_in,
    resp_out,
    resp_in,
    den_out,
    den_in,
    numer,
    spread,
    update,
    sums,
    tile_out,
    tile_in,
    tiles,
    tiles_t,
    in_sem,
    count_send,
    count_recv,
    relay_send,
    relay_recv,
    resp_send,
    resp_recv,
    den_send,
    den_recv,
    fan_send,
    fan_recv,
):
    me = lax.axis_index("orient")
    mine = lax.axis_index("frame")
    rot_rows, pixels = logt.shape
    frame_rows = frames.shape[0]
    group_blocks = index_ref.shape[1]
    tile_rows, width = prior_ref.shape[1:]
    columns = pixels // n_frame
    tile_count = tile_rows * n_orient
    chunk = (384 // tile_rows if n_orient % max(384 // tile_rows, 1) == 0 else 1) * tile_rows
    partner = me + 1 - 2 * lax.rem(me, 2)
    across = me + 2 - 4 * lax.rem(me // 2, 2)
    fourth = frame_rows // 4

    def fan_out(send):
        if n_orient <= 32:
            for d in sorted(range(1, n_orient), key=lambda d: abs(2 * d - n_orient)):
                send(d, 0)
        else:
            lax.fori_loop(1, n_orient, send, 0)

    part = fourth // PARTS

    logt_copy = pltpu.make_async_copy(logt_hbm, logt, in_sem.at[0])
    logt_copy.start()
    step = frame_rows // PARTS
    frame_copies = []
    for c in range(PARTS):
        rows = pl.ds(c * step, step)
        copy = pltpu.make_async_copy(frames_hbm.at[rows], frames.at[rows], in_sem.at[1 + c])
        copy.start()
        frame_copies.append(copy)

    small_copies = []
    for i, (source, target) in enumerate(
        ((index_hbm, index_ref), (weight_hbm, weight_ref), (prior_hbm, prior_ref))
    ):
        copy = pltpu.make_async_copy(source, target, in_sem.at[1 + PARTS + i])
        copy.start()
        small_copies.append(copy)

    barrier = pltpu.get_barrier_semaphore()

    def greet(d, carry):
        pl.semaphore_signal(
            barrier, inc=1, device_id={"orient": lax.rem(me + d, n_orient)}, device_id_type=MESH
        )
        return carry

    fan_out(greet)
    for d in range(1, n_frame):
        pl.semaphore_signal(
            barrier, inc=1, device_id={"frame": lax.rem(mine + d, n_frame)}, device_id_type=MESH
        )

    for c in range(PARTS):
        frame_copies[c].wait()
        counts[c * step : (c + 1) * step] = (
            frames[c * step : (c + 1) * step].astype(F32).astype(BF16)
        )
    logt_copy.wait()
    mass = jnp.zeros((rot_rows, 128), F32)
    for c in range(pixels // 512):
        value = jnp.exp(logt[:, c * 512 : (c + 1) * 512].astype(F32))
        intensity[:, c * 512 : (c + 1) * 512] = value
        for k in range(4):
            mass = mass + value[:, k * 128 : (k + 1) * 128]
    mass = jnp.sum(mass, axis=1, keepdims=True)
    correlation = lax.dot_general(
        logt[...], counts[...], (((1,), (1,)), ((), ())), preferred_element_type=F32
    )
    score = (64.0 / pixels) * (correlation - mass)
    scores[...] = score
    peak = jnp.max(score, axis=0, keepdims=True)
    stat_mine[0:1, :] = peak
    stat_mine[1:2, :] = jnp.sum(jnp.exp(score - peak), axis=0, keepdims=True)

    pl.semaphore_wait(barrier, n_orient - 1 + n_frame - 1)

    def send_stat(d, carry):
        remote(
            stat_mine,
            stat_in.at[d - 1],
            fan_send.at[0],
            fan_recv.at[0],
            {"orient": lax.rem(me + d, n_orient)},
        ).start()
        return carry

    fan_out(send_stat)

    def quarter(owner, c):
        return pl.ds(pl.multiple_of(lax.rem(owner, 4) * fourth + c * part, 16), part)

    count_copies = []
    for c in range(PARTS):
        for d in range(1, n_frame):
            to = lax.rem(mine + d, n_frame)
            copy = remote(
                counts.at[quarter(me, c), pl.ds(pl.multiple_of(to * columns, 128), columns)],
                other.at[d - 1, quarter(me, c)],
                count_send.at[d - 1, c],
                count_recv.at[d - 1, c],
                {"frame": to},
            )
            copy.start()
            count_copies.append((d, c, copy))

    for copy in small_copies:
        copy.wait()

    weight_low = weight_ref[...].astype(BF16).astype(F32)
    index = index_ref[...]
    lane = lax.broadcasted_iota(jnp.int32, (8, 128), 1)
    joint = spread.shape[1] // tile_rows
    strip = joint * tile_rows

    def build(o, carry):
        first = o * strip
        row_id = lax.broadcasted_iota(jnp.int32, (strip, rot_rows), 0) + first
        total = jnp.zeros((strip, rot_rows), F32)
        for j in range(group_blocks):
            value = jnp.where(row_id == index[0, j][None, :], weight_low[0, j][None, :], 0.0)
            value = value + jnp.where(
                row_id == index[1, j][None, :], weight_low[1, j][None, :], 0.0
            )
            low = value.astype(BF16)
            total = total + low.astype(F32)
            spread[o, :, j * rot_rows : (j + 1) * rot_rows] = low
        weight_sum = jnp.sum(total, axis=1, keepdims=True)
        for i in range(joint):
            packed = jnp.zeros((8, 128), F32)
            for b in range(tile_rows // 8):
                at = i * tile_rows + b * 8
                exact = weight_sum[at : at + 8]
                high = exact.astype(BF16).astype(F32)
                packed = packed + jnp.where(lane == b, high, 0.0)
                packed = packed + jnp.where(lane == 64 + b, exact - high, 0.0)
            sums[o * joint + i] = packed
        return carry

    lax.fori_loop(0, n_orient // joint, build, 0)

    relay_copies = []

    def relay(owner, d, c, kind, to):
        where = other.at[d - 1, quarter(owner, c)]
        copy = remote(
            where,
            where,
            relay_send.at[kind, d - 1, c],
            relay_recv.at[kind, d - 1, c],
            {"orient": to},
        )
        copy.start()
        relay_copies.append((kind, d, c, copy))

    def relay_first(start, stop):
        for d, c, copy in count_copies:
            if start <= c < stop:
                copy.wait_recv()
                relay(me, d, c, 0, across)
                relay(me, d, c, 1, partner)

    def relay_second(start, stop):
        for kind, d, c, copy in list(relay_copies):
            if kind == 0 and start <= c < stop:
                copy.wait_recv()
                relay(across, d, c, 2, partner)

    relay_first(0, 2)

    fan_wait_recv = pltpu.make_async_copy(stat_in, stat_in, fan_recv.at[0])
    fan_wait_send = pltpu.make_async_copy(stat_in, stat_in, fan_send.at[0])
    fan_wait_recv.wait()
    peaks = stat_in[:, 0, :]
    totals = stat_in[:, 1, :]
    peak_mine = stat_mine[0:1, :]
    peak = jnp.maximum(jnp.max(peaks, axis=0, keepdims=True), peak_mine)
    total = stat_mine[1:2, :] * jnp.exp(peak_mine - peak) + jnp.sum(
        totals * jnp.exp(peaks - peak), axis=0, keepdims=True
    )
    evidence_ref[...] = peak + jnp.log(total)
    resp = jnp.exp(scores[...] - peak) / total
    resp_out[...] = resp.astype(BF16)
    den = jnp.sum(resp, axis=1, keepdims=True).astype(BF16)
    den_out[...] = jnp.broadcast_to(den, (rot_rows, 128))

    resp_copies = []
    for d in range(1, n_frame):
        to = {"frame": lax.rem(mine + d, n_frame)}
        copy = remote(resp_out, resp_in.at[d - 1], resp_send.at[d - 1], resp_recv.at[d - 1], to)
        copy.start()
        den_copy = remote(den_out, den_in.at[d - 1], den_send.at[d - 1], den_recv.at[d - 1], to)
        den_copy.start()
        resp_copies.append((copy, den_copy))
    fan_wait_send.wait()

    span = min(columns, 512)
    first = pl.multiple_of(mine * columns, 128)
    pieces = columns // span

    def own_sums(start, stop):
        for c in range(start, stop):
            mixed = jnp.dot(
                resp_out[...],
                counts[:, pl.ds(pl.multiple_of(first + c * span, 128), span)],
                preferred_element_type=F32,
            )
            numer[:, c * span : (c + 1) * span] = mixed.astype(BF16).astype(F32)

    relay_first(2, 3)
    own_sums(0, pieces // 2)
    relay_first(3, PARTS)
    relay_second(0, 2)
    own_sums(pieces // 2, pieces)
    relay_second(2, PARTS)
    for copy, den_copy in resp_copies:
        copy.wait_recv()
        den_copy.wait_recv()
    for kind, d, c, copy in relay_copies:
        if kind > 0:
            copy.wait_recv()

    share = frame_rows * n_frame / (rot_rows * n_orient)
    den_all = den_out[...].astype(F32)
    for d in range(1, n_frame):
        den_all = den_all + den_in[d - 1].astype(F32)
    inverse = 1.0 / (den_all + share)
    for c in range(columns // span):
        cols = slice(c * span, (c + 1) * span)
        value = numer[:, cols]
        for d in range(1, n_frame):
            mixed = jnp.dot(resp_in[d - 1], other[d - 1, :, cols], preferred_element_type=F32)
            value = value + mixed.astype(BF16).astype(F32)
        value = value + share * intensity[:, pl.ds(pl.multiple_of(first + c * span, 128), span)]
        for k in range(span // width):
            j = c * (span // width) + k
            new = value[:, k * width : (k + 1) * width] * inverse
            high = new.astype(BF16)
            update[j * rot_rows : (j + 1) * rot_rows, 0:width] = high
            update[j * rot_rows : (j + 1) * rot_rows, width : 2 * width] = (
                new - high.astype(F32)
            ).astype(BF16)

    owners = chunk // tile_rows

    def gather_in(c, carry):
        block = spread[pl.ds(c * (chunk // strip), chunk // strip)].reshape(chunk, group_blocks * rot_rows)
        summed = jnp.dot(block, update[...], preferred_element_type=F32)
        summed = summed[:, 0:width] + summed[:, width : 2 * width]
        for i in range(owners):
            own = summed[i * tile_rows : (i + 1) * tile_rows]
            message = jnp.concatenate([own, sums[c * owners + i]], axis=0)
            tile_out[c * owners + i] = message.astype(BF16)
        return carry

    lax.fori_loop(0, tile_count // chunk, gather_in, 0)

    def send_tiles(d, carry):
        to = lax.rem(me + d, n_orient)
        remote(
            tile_out.at[to], tile_in.at[d - 1], fan_send.at[1], fan_recv.at[1], {"orient": to}
        ).start()
        return carry

    fan_out(send_tiles)
    pltpu.make_async_copy(tile_in, tile_in, fan_recv.at[1]).wait()
    whole = lax.fori_loop(0, n_orient - 1, lambda d, so_far: so_far + tile_in[d].astype(F32), tile_out[me].astype(F32))
    prior_weight = rot_rows * group_blocks / (4.0 * tile_rows)
    weight = [
        whole[tile_rows:, b : b + 1] + whole[tile_rows:, 64 + b : 65 + b]
        for b in range(tile_rows // 8)
    ]
    weight = jnp.concatenate(weight, axis=0)
    value = whole[0:tile_rows] + prior_weight * prior_ref[0]
    value = value / (weight + prior_weight)
    volume_ref[0] = value
    tiles[me] = (value - 1.0).astype(BF16)

    def send_volume(d, carry):
        own = tiles.at[me]
        remote(
            own, own, fan_send.at[2], fan_recv.at[2], {"orient": lax.rem(me + d, n_orient)}
        ).start()
        return carry

    fan_out(send_volume)
    for d, c, copy in count_copies:
        copy.wait_send()
    for kind, d, c, copy in relay_copies:
        copy.wait_send()
    for copy, den_copy in resp_copies:
        copy.wait_send()
        den_copy.wait_send()
    pltpu.make_async_copy(tile_in, tile_in, fan_send.at[1]).wait()
    incoming = tiles.at[pl.ds(0, n_orient - 1)]
    pltpu.make_async_copy(incoming, incoming, fan_recv.at[2]).wait()

    def turn(c, carry):
        value = tiles[pl.ds(c * owners, owners)].astype(F32).reshape(chunk, width)
        tiles_t[:, pl.ds(pl.multiple_of(c * chunk, 128), chunk)] = value.T.astype(BF16)
        return carry

    lax.fori_loop(0, tile_count // chunk, turn, 0)
    both = weight_low[0] + weight_low[1]
    both = jnp.where(index[0] == index[1], both.astype(BF16).astype(F32), both)
    scale = 1.0 / both
    pair = 2 if group_blocks % 2 == 0 else 1
    for c in range(group_blocks // pair):
        cols = slice(c * pair * rot_rows, (c + 1) * pair * rot_rows)
        block = spread[:, :, cols].reshape(tile_count, pair * rot_rows)
        blended = jnp.dot(tiles_t[...], block, preferred_element_type=F32)
        for k in range(pair):
            j = c * pair + k
            value = blended[:, k * rot_rows : (k + 1) * rot_rows] * scale[j][None, :]
            value = jnp.log(1.0 + value)
            new_log_ref[:, j * width : (j + 1) * width] = value.T.astype(BF16)
    pltpu.make_async_copy(incoming, incoming, fan_send.at[2]).wait()


def place(a_in, b_in, c_in, a_out, b_out, c_out, sem):
    copies = [
        pltpu.make_async_copy(source, target, sem.at[i])
        for i, (source, target) in enumerate(((a_in, a_out), (b_in, b_out), (c_in, c_out)))
    ]
    for copy in copies:
        copy.start()
    for copy in copies:
        copy.wait()


def on_device(log_tomograms, frames, tile_index, tile_weight, prior_volume):
    n_orient = lax.axis_size("orient")
    n_frame = lax.axis_size("frame")
    rot_rows, pixels = log_tomograms.shape
    frame_rows = frames.shape[0]
    group_blocks = tile_index.shape[1]
    tile_rows, width = prior_volume.shape[1:]
    columns = pixels // n_frame
    tile_count = tile_rows * n_orient
    others = max(n_frame - 1, 1)
    dma = pltpu.SemaphoreType.DMA
    vmem = pl.BlockSpec(memory_space=pltpu.VMEM)
    hbm = pl.BlockSpec(memory_space=pltpu.HBM)
    new_log, volume, evidence = pl.pallas_call(
        functools.partial(kernel, n_orient, n_frame),
        out_shape=(
            pltpu.VMEM((rot_rows, columns), BF16),
            pltpu.VMEM((1, tile_rows, width), F32),
            pltpu.VMEM((1, frame_rows), F32),
        ),
        in_specs=[hbm] * 5,
        out_specs=(vmem, vmem, vmem),
        scratch_shapes=[
            pltpu.VMEM((rot_rows, pixels), BF16),
            pltpu.VMEM((frame_rows, pixels), jnp.int32),
            pltpu.VMEM(tile_index.shape, jnp.int32),
            pltpu.VMEM(tile_weight.shape, F32),
            pltpu.VMEM(prior_volume.shape, F32),
            pltpu.VMEM((frame_rows, pixels), BF16),
            pltpu.VMEM((others, frame_rows, columns), BF16),
            pltpu.VMEM((rot_rows, pixels), F32),
            pltpu.VMEM((rot_rows, frame_rows), F32),
            pltpu.VMEM((2, frame_rows), F32),
            pltpu.VMEM((n_orient - 1, 2, frame_rows), F32),
            pltpu.VMEM((rot_rows, frame_rows), BF16),
            pltpu.VMEM((others, rot_rows, frame_rows), BF16),
            pltpu.VMEM((rot_rows, 128), BF16),
            pltpu.VMEM((others, rot_rows, 128), BF16),
            pltpu.VMEM((rot_rows, columns), F32),
            pltpu.VMEM((n_orient // 2, 2 * tile_rows, group_blocks * rot_rows), BF16),
            pltpu.VMEM((group_blocks * rot_rows, 2 * width), BF16),
            pltpu.VMEM((n_orient, 8, width), F32),
            pltpu.VMEM((n_orient, tile_rows + 8, width), BF16),
            pltpu.VMEM((n_orient - 1, tile_rows + 8, width), BF16),
            pltpu.VMEM((n_orient, tile_rows, width), BF16),
            pltpu.VMEM((width, tile_count), BF16),
            dma((4 + PARTS,)),
            dma((others, PARTS)),
            dma((others, PARTS)),
            dma((3, others, PARTS)),
            dma((3, others, PARTS)),
            dma((others,)),
            dma((others,)),
            dma((others,)),
            dma((others,)),
            dma((3,)),
            dma((3,)),
        ],
        compiler_params=pltpu.CompilerParams(
            collective_id=0, has_side_effects=True, vmem_limit_bytes=48 * 1024 * 1024
        ),
    )(*(
        pltpu.with_memory_space_constraint(value, pltpu.HBM)
        for value in (log_tomograms, frames, tile_index, tile_weight, prior_volume)
    ))
    made = (new_log, volume, evidence)
    new_log, volume, evidence = pl.pallas_call(
        place,
        out_shape=tuple(jax.ShapeDtypeStruct(value.shape, value.dtype) for value in made),
        in_specs=[vmem] * 3,
        out_specs=(hbm,) * 3,
        scratch_shapes=[dma((3,))],
        compiler_params=pltpu.CompilerParams(vmem_limit_bytes=4 * 1024 * 1024),
    )(*made)
    return (new_log, volume, evidence.reshape(frame_rows))


def solution(mesh):
    placed = (
        P("orient", None),
        P("frame", None),
        P(None, "frame", "orient"),
        P(None, "frame", "orient"),
        P("frame", "orient", None),
    )
    return jax.shard_map(
        on_device,
        mesh=mesh,
        in_specs=placed,
        out_specs=(P("orient", "frame"), P("frame", "orient", None), P("frame")),
        check_vma=False,
    )
```
